32 devices in a mesh: depth: 8 (over y, x, core), area: 4 (over z).
Axes of the slice: x: 2, y: 2, z: 4, core: 2. Of those that a mesh axis runs over, the one named last changes fastest.
Arguments:
- rhs_field: float32 [16, 32, 2048], P('depth', None, 'area'), may hold values from -8 to 8
- start_field: float32 [16, 32, 2048], P('depth', None, 'area'), may hold values from -4 to 4
- inverses: float32 [16, 2048, 512], P('depth', 'area'), may hold values from -0.044194174 to 1
- facies: int32 [16, 2048], P('depth', 'area'), may hold values from 0 to 7
- neighbours: int32 [2048, 4], P('area'), may hold values from 0 to 639, as said below
- lateral_table: float32 [8, 4], replicated, may hold values from 0.05 to 0.3
- vertical_table: float32 [8], replicated, may hold values from 0.9 to 1
Outputs:
- updated: float32 [16, 32, 2048], P('depth', None, 'area')
The draws below stay inside these ranges and needn't reach their ends.
Inputs may be any that keep to these rules, and one draw needn't show every extreme that they name: `neighbours`: index 64 + c is column c itself; entries 0 and 1 of column c are c - 1 and c + 1, the others lie within 64 columns of c and differ from it.
All inputs are finite; a program needn't handle non-finite values.
Results may differ from the reference program's by a relative error of at most 0.00016.
Values sent between devices are 32-bit elements; how exact they have to be, the bound alone decides.
No kernel may reach another device: no remote copies, remote signals or barrier semaphores. Data moves between devices by JAX's collectives and lax.ppermute only.
A program may use at most 128 MiB of HBM per device.

```python
import math
import jax
import jax.numpy as jnp
from jax import lax

CELLS = 512
RHS = 32
HW = 64
NBRS = 4
FACIES = 8
LAYERS = 16
NCELLS = 2048


def draw_neighbours(key, part):
    cell = jnp.arange(NCELLS, dtype=jnp.int32) % CELLS
    first, second = jax.random.split(jax.random.fold_in(key, 11))
    reach = jax.random.randint(first, (NCELLS, NBRS - 2), 1, HW + 1)
    sign = jax.random.randint(second, (NCELLS, NBRS - 2), 0, 2) * 2 - 1
    left = jnp.full((NCELLS, 1), -1, jnp.int32)
    right = jnp.full((NCELLS, 1), 1, jnp.int32)
    offsets = jnp.concatenate([left, right, reach * sign], axis=1)
    return (HW + cell[:, None] + offsets).astype(jnp.int32)


def draw_inverses(key, part):
    first, second = jax.random.split(jax.random.fold_in(key, 23))
    blocks = NCELLS // CELLS
    diag = jnp.exp(jax.random.uniform(first, (LAYERS, blocks, CELLS), jnp.float32, math.log(0.9), 0.0))
    eye = jnp.eye(CELLS, dtype=jnp.float32)
    off = jnp.clip(jax.random.normal(second, (LAYERS, blocks, CELLS, CELLS), jnp.float32), -4.0, 4.0) * (0.25 / math.sqrt(CELLS))
    whole = off * (1.0 - eye)[None, None] + eye[None, None] * diag[..., None]
    return whole.reshape(LAYERS, NCELLS, CELLS)


def place_ends(values, key, least, high):
    longest = values.shape.index(max(values.shape))
    spots = []
    for shift in (0, 1):
        where = [jax.random.randint(jax.random.fold_in(key, axis), (), 0, length) for axis, length in enumerate(values.shape)]
        where[longest] = (where[longest] + shift) % values.shape[longest]
        spots.append(tuple(where))
    return values.at[spots[0]].set(least).at[spots[1]].set(high)


def steps_of(key, shape, shards, smallest, high):
    loudness = 1.0
    for dim, shards_of in shards:
        heights = jax.random.uniform(jax.random.fold_in(jax.random.fold_in(key, 6), dim), (shards_of,), jnp.float32, smallest / len(shards), high / len(shards))
        loudness = loudness * jnp.repeat(jnp.exp(heights), shape[dim] // shards_of).reshape((-1,) + (1,) * (len(shape) - 1 - dim))
    return loudness


def noise(own_key, extent, width, most, pieces=(), kind=jnp.bfloat16):
    array = width * jax.random.normal(own_key, extent, jnp.float32)
    if pieces:
        array = array * steps_of(own_key, extent, pieces, -0.22, 0.18)
    return jnp.clip(array, -most, most).astype(kind)


def setup_inputs(seed: int = 0) -> dict:
    streams_of = jax.random.split(jax.random.key(seed), 8)
    return {
        "rhs_field": noise(streams_of[0], (LAYERS, RHS, NCELLS), 1.0, 8.0, ((0, 8), (2, 4)), jnp.float32),
        "start_field": noise(streams_of[1], (LAYERS, RHS, NCELLS), 0.5, 4.0, ((0, 8), (2, 4)), jnp.float32),
        "inverses": draw_inverses(jax.random.fold_in(streams_of[7], 71), 0),
        "facies": place_ends(jax.random.randint(streams_of[3], (LAYERS, NCELLS), 0, FACIES), jax.random.fold_in(streams_of[3], 1), 0, FACIES - 1).astype(jnp.int32),
        "neighbours": draw_neighbours(jax.random.fold_in(streams_of[7], 71), 0),
        "lateral_table": jnp.clip(jnp.exp(jax.random.uniform(streams_of[5], (FACIES, NBRS), jnp.float32, math.log(0.05), math.log(0.3))), 0.05, 0.3),
        "vertical_table": jnp.clip(jnp.exp(jax.random.uniform(streams_of[6], (FACIES,), jnp.float32, math.log(0.9), math.log(1.0))), 0.9, 1.0),
    }


def apply_blocks(field, blocks):
    parts = field.reshape(field.shape[0], -1, CELLS)
    mats = blocks.reshape(-1, CELLS, CELLS)
    return jnp.einsum("rac,acd->rad", parts, mats, precision=lax.Precision.HIGHEST).reshape(field.shape)


def apply_blocks_t(field, blocks):
    parts = field.reshape(field.shape[0], -1, CELLS)
    mats = blocks.reshape(-1, CELLS, CELLS)
    return jnp.einsum("rad,acd->rac", parts, mats, precision=lax.Precision.HIGHEST).reshape(field.shape)


def lateral(field, facies, neighbours, lateral_table):
    starts = (jnp.arange(NCELLS, dtype=jnp.int32) // CELLS * CELLS)[:, None]
    index = (starts + neighbours).astype(jnp.int32)

    def one_layer(pair):
        layer, kinds = pair
        padded = jnp.pad(layer, ((0, 0), (HW, HW)))
        values = padded[:, index]
        weight = lateral_table[kinds]
        return jnp.sum(weight[None] * (layer[:, :, None] - values), axis=-1)

    return lax.map(one_layer, (field, facies))


def reference(rhs_field, start_field, inverses, facies, neighbours, lateral_table, vertical_table):
    vert = vertical_table[facies]
    zero_layer = jnp.zeros((1, RHS, NCELLS), jnp.float32)
    upper = jnp.concatenate([vert[1:, None, :] * start_field[1:], zero_layer], axis=0)
    g = rhs_field - lateral(start_field, facies, neighbours, lateral_table) + upper

    def down(carry, item):
        g_k, vert_k, inv_k = item
        y_k = apply_blocks(g_k + vert_k[None] * carry, inv_k)
        return y_k, y_k

    _, y = lax.scan(down, jnp.zeros((RHS, NCELLS), jnp.float32), (g, vert, inverses))
    y_prev = jnp.concatenate([zero_layer, y[:-1]], axis=0)
    h = rhs_field - lateral(y, facies, neighbours, lateral_table) + vert[:, None, :] * y_prev

    def upward(carry, item):
        h_k, vert_k, inv_k = item
        z_k = apply_blocks_t(h_k + carry, inv_k)
        return vert_k[None] * z_k, z_k

    _, updated = lax.scan(upward, jnp.zeros((RHS, NCELLS), jnp.float32), (h, vert, inverses), reverse=True)
    return updated
```

```python
import functools

import jax
import jax.numpy as jnp
from jax import lax
from jax.experimental import pallas as pl
from jax.experimental.pallas import tpu as pltpu
from jax.sharding import PartitionSpec as P

F32 = jnp.float32
BF16 = jnp.bfloat16
HW = 64
LANES = 128
NN = (((1,), (0,)), ((), ()))
NT = (((1,), (1,)), ((), ()))

VMEM = pl.BlockSpec(memory_space=pltpu.VMEM)
SMEM = pl.BlockSpec(memory_space=pltpu.SMEM)


def call(body, name, out_shape, in_specs, limit, flops, moved, scratch=()):
    return pl.pallas_call(
        body,
        name=name,
        out_shape=out_shape,
        in_specs=in_specs,
        out_specs=jax.tree.map(lambda _: VMEM, out_shape),
        scratch_shapes=list(scratch),
        compiler_params=pltpu.CompilerParams(vmem_limit_bytes=limit << 20),
        cost_estimate=pl.CostEstimate(flops=flops, bytes_accessed=moved, transcendentals=0),
    )


def sds(shape, dtype=F32):
    return jax.ShapeDtypeStruct(shape, dtype)


def split(value):
    high = value.astype(BF16)
    return high, (value - high.astype(F32)).astype(BF16)


def times(value, high, low, dims=NN):
    rows = value.shape[0]
    value_high, value_low = split(value)
    both = lax.dot_general(
        jnp.concatenate([value_high, value_low], axis=0), high, dims, preferred_element_type=F32
    )
    rest = lax.dot_general(value_high, low, dims, preferred_element_type=F32)
    return both[:rows] + (both[rows:] + rest)


def looked_up(kinds, entry, count):
    value = jnp.full(kinds.shape, entry(0), F32)
    for kind in range(1, count):
        value = jnp.where(kinds == kind, entry(kind), value)
    return value


def edges_kernel(start_ref, facies_ref, vertical_ref, left_ref, right_ref, top_ref):
    layers, _, width = start_ref.shape
    left_ref[...] = jnp.concatenate([start_ref[k, :, :HW] for k in range(layers)], axis=1)
    right_ref[...] = jnp.concatenate([start_ref[k, :, width - HW :] for k in range(layers)], axis=1)
    vert = looked_up(facies_ref[0:1, :], lambda kind: vertical_ref[kind], vertical_ref.shape[0])
    top_ref[...] = vert * start_ref[0]


def setup_kernel(inverses_ref, facies_ref, lateral_ref, vertical_ref,
                 high_ref, low_ref, product_ref, product_high_ref, product_low_ref,
                 weight_ref, vert_ref):
    layers, width, _ = inverses_ref.shape
    kinds = facies_ref[...]
    vert = looked_up(kinds, lambda kind: vertical_ref[kind], vertical_ref.shape[0])
    vert_ref[...] = vert
    for slot in range(lateral_ref.shape[1]):
        weight_ref[slot] = looked_up(kinds, lambda kind: lateral_ref[kind, slot], lateral_ref.shape[0])
    step = LANES
    for layer in range(layers):
        for row in range(0, width, step):
            rows = slice(row, row + step)
            high_ref[layer, rows, :], low_ref[layer, rows, :] = split(inverses_ref[layer, rows, :])
    for row in range(0, width, step):
        rows = slice(row, row + step)
        value = inverses_ref[0, rows, :]
        for layer in range(1, layers):
            value = times(value * vert[layer : layer + 1], high_ref[layer], low_ref[layer])
        scale = jnp.transpose(jnp.broadcast_to(vert[0:1, rows], (step, step)))
        value = value * jnp.concatenate([scale] * (width // step), axis=1)
        product_ref[rows, :] = value
        product_high_ref[rows, :], product_low_ref[rows, :] = split(value)


def pair_kernel(bit_of, own_ref, own_high_ref, own_low_ref, other_ref,
                other_high_ref, other_low_ref, product_ref, product_high_ref, product_low_ref):
    width = own_ref.shape[0]
    step = LANES
    for row in range(0, width, step):
        rows = slice(row, row + step)
        other_high_ref[rows, :], other_low_ref[rows, :] = split(other_ref[rows, :])
    upper = bit_of()

    def multiply(left_ref, right_high_ref, right_low_ref):
        for row in range(0, width, step):
            rows = slice(row, row + step)
            value = times(left_ref[rows, :], right_high_ref[...], right_low_ref[...])
            product_ref[rows, :] = value
            product_high_ref[rows, :], product_low_ref[rows, :] = split(value)

    @pl.when(upper == 1)
    def _():
        multiply(other_ref, own_high_ref, own_low_ref)

    @pl.when(upper == 0)
    def _():
        multiply(own_ref, other_high_ref, other_low_ref)


def split_kernel(value_ref, high_ref, low_ref):
    for row in range(0, value_ref.shape[0], LANES):
        rows = slice(row, row + LANES)
        high_ref[rows, :], low_ref[rows, :] = split(value_ref[rows, :])


def lateral(values, low, high, neighbours_ref, weight_ref):
    layers = len(values)
    rows, width = values[0].shape
    slots = neighbours_ref.shape[0]
    extended = [
        jnp.concatenate(
            [low[:, k * HW : (k + 1) * HW], values[k], high[:, k * HW : (k + 1) * HW]], axis=1
        )
        for k in range(layers)
    ]
    result = []
    for k in range(layers):
        blocks = []
        for block in range(width // LANES):
            lanes = slice(block * LANES, (block + 1) * LANES)
            first = extended[k][:, block * LANES : (block + 1) * LANES]
            second = extended[k][:, (block + 1) * LANES : (block + 2) * LANES]
            here = values[k][:, lanes]
            total = jnp.zeros((rows, LANES), F32)
            for slot in range(slots):
                index = neighbours_ref[slot : slot + 1, lanes] - block * LANES
                index = jnp.broadcast_to(index, (rows, LANES))
                inner = index & (LANES - 1)
                taken = jnp.where(
                    index < LANES,
                    jnp.take_along_axis(first, inner, axis=1, mode="promise_in_bounds"),
                    jnp.take_along_axis(second, inner, axis=1, mode="promise_in_bounds"),
                )
                total += weight_ref[slot, k : k + 1, lanes] * (here - taken)
            blocks.append(total)
        result.append(jnp.concatenate(blocks, axis=1))
    return result


def masked(flag, value):
    return jnp.where(flag, value, jnp.zeros_like(value))


def first_kernel(place, start_ref, rhs_ref, low_ref, high_ref, below_ref, neighbours_ref, weight_ref,
                 vert_ref, inv_high_ref, inv_low_ref, g_ref, total_ref):
    layers = start_ref.shape[0]
    depth, depths, area, areas = place()
    low = masked(area > 0, low_ref[...])
    high = masked(area < areas - 1, high_ref[...])
    below = masked(depth < depths - 1, below_ref[...])
    start = [start_ref[k] for k in range(layers)]
    lat = lateral(start, low, high, neighbours_ref, weight_ref)
    carried = None
    for k in range(layers):
        upper = vert_ref[k + 1 : k + 2, :] * start[k + 1] if k + 1 < layers else below
        g = rhs_ref[k] - lat[k] + upper
        g_ref[k] = g
        if carried is not None:
            g = g + vert_ref[k : k + 1, :] * carried
        carried = times(g, inv_high_ref[k], inv_low_ref[k])
    total_ref[...] = carried


def join_kernel(bit_of, up, own_ref, other_ref, own_high_ref, own_low_ref, other_high_ref,
                other_low_ref, total_ref):
    dims = NT if up else NN
    last = bit_of() == (0 if up else 1)

    @pl.when(last)
    def _():
        total_ref[...] = own_ref[...] + times(other_ref[...], own_high_ref[...], own_low_ref[...], dims)

    @pl.when(jnp.logical_not(last))
    def _():
        total_ref[...] = other_ref[...] + times(own_ref[...], other_high_ref[...], other_low_ref[...], dims)


def entering(bits, up, heard, products):
    value = None
    for level in reversed(range(len(heard))):
        later = bits[level] == (0 if up else 1)
        if value is None:
            value = masked(later, heard[level])
        else:
            high, low = products[level]
            value = jnp.where(
                later, heard[level] + times(value, high[...], low[...], NT if up else NN), value
            )
    return value


def down_kernel(bits_of, levels, g_ref, vert_ref, inv_high_ref, inv_low_ref, *refs):
    heard, refs = refs[:levels], refs[levels:]
    products, refs = refs[: 2 * (levels - 1)], refs[2 * (levels - 1) :]
    y_ref, entering_ref, left_ref, right_ref = refs
    layers, _, width = g_ref.shape
    pairs = [(products[2 * i], products[2 * i + 1]) for i in range(levels - 1)]
    carried = entering(bits_of(), False, [ref[...] for ref in heard], pairs)
    entering_ref[...] = carried
    for k in range(layers):
        carried = times(
            g_ref[k] + vert_ref[k : k + 1, :] * carried, inv_high_ref[k], inv_low_ref[k]
        )
        y_ref[k] = carried
    left_ref[...] = jnp.concatenate([y_ref[k, :, :HW] for k in range(layers)], axis=1)
    right_ref[...] = jnp.concatenate([y_ref[k, :, width - HW :] for k in range(layers)], axis=1)


def turn_kernel(place, y_ref, entering_ref, rhs_ref, low_ref, high_ref, neighbours_ref, weight_ref,
                vert_ref, inv_high_ref, inv_low_ref, h_ref, total_ref):
    layers = y_ref.shape[0]
    _, _, area, areas = place()
    low = masked(area > 0, low_ref[...])
    high = masked(area < areas - 1, high_ref[...])
    values = [y_ref[k] for k in range(layers)]
    lat = lateral(values, low, high, neighbours_ref, weight_ref)
    carried = None
    for k in reversed(range(layers)):
        vert = vert_ref[k : k + 1, :]
        h = rhs_ref[k] - lat[k] + vert * (values[k - 1] if k else entering_ref[...])
        h_ref[k] = h
        carried = vert * times(h if carried is None else h + carried, inv_high_ref[k], inv_low_ref[k], NT)
    total_ref[...] = carried


def up_kernel(bits_of, levels, h_ref, vert_ref, inv_high_ref, inv_low_ref, *refs):
    heard, refs = refs[:levels], refs[levels:]
    products, refs = refs[: 2 * (levels - 1)], refs[2 * (levels - 1) :]
    (updated_ref,) = refs
    layers = h_ref.shape[0]
    pairs = [(products[2 * i], products[2 * i + 1]) for i in range(levels - 1)]
    carried = entering(bits_of(), True, [ref[...] for ref in heard], pairs)
    for k in reversed(range(layers)):
        value = times(h_ref[k] + carried, inv_high_ref[k], inv_low_ref[k], NT)
        updated_ref[k] = value
        carried = vert_ref[k : k + 1, :] * value


def shards(rhs_field, start_field, inverses, facies, neighbours, lateral_table, vertical_table):
    layers, count, width = rhs_field.shape
    slots = neighbours.shape[1]
    depths, areas = lax.axis_size("depth"), lax.axis_size("area")
    levels = depths.bit_length() - 1
    assert depths == 1 << levels and levels >= 2

    def bit(level):
        return (lax.axis_index("depth") >> level) & 1

    def bits():
        return [bit(level) for level in range(levels)]

    def place():
        return lax.axis_index("depth"), depths, lax.axis_index("area"), areas

    def swapped(value, level):
        return lax.ppermute(value, "depth", [(i, i ^ (1 << level)) for i in range(depths)])

    def from_sides(left, right):
        low = lax.ppermute(right, "area", [(i, (i + 1) % areas) for i in range(areas)])
        high = lax.ppermute(left, "area", [((i + 1) % areas, i) for i in range(areas)])
        return low, high

    field = sds((layers, count, width))
    row = sds((count, width))
    matrix, matrix16 = sds((width, width)), sds((width, width), BF16)
    edge = sds((count, layers * HW))
    flops = 2 * width * width
    neighbour_rows = neighbours.T

    left, right, top = call(
        edges_kernel, "edges", (edge, edge, row), [VMEM, VMEM, SMEM], 4, 1 << 16, 1 << 18
    )(start_field, facies, vertical_table)
    low, high = from_sides(left, right)
    below = lax.ppermute(top, "depth", [((i + 1) % depths, i) for i in range(depths)])

    inv16 = sds((layers, width, width), BF16)
    inv_high, inv_low, product, product_high, product_low, weight, vert = call(
        setup_kernel, "setup",
        (inv16, inv16, matrix, matrix16, matrix16, sds((slots, layers, width)), sds((layers, width))),
        [VMEM, VMEM, SMEM, SMEM], 16, 3 * (layers - 1) * flops * width, 8 << 20,
    )(inverses, facies, lateral_table, vertical_table)

    own = [(product_high, product_low)]
    other = []
    for level in range(levels - 1):
        arrived = swapped(product, level)
        if level < levels - 2:
            other_high, other_low, product, product_high, product_low = call(
                functools.partial(pair_kernel, functools.partial(bit, level)), f"pair{level}",
                (matrix16, matrix16, matrix, matrix16, matrix16), [VMEM] * 4, 16,
                3 * flops * width, 6 << 20,
            )(product, product_high, product_low, arrived)
            own.append((product_high, product_low))
        else:
            other_high, other_low = call(
                split_kernel, f"split{level}", (matrix16, matrix16), [VMEM], 8, 1 << 20, 2 << 20
            )(arrived)
        other.append((other_high, other_low))

    g, total = call(
        functools.partial(first_kernel, place), "first", (field, row), [VMEM] * 10, 8,
        3 * layers * count * flops, 4 << 20,
    )(start_field, rhs_field, low, high, below, neighbour_rows, weight, vert, inv_high, inv_low)

    def exchange(total, up):
        heard = []
        for level in range(levels):
            heard.append(swapped(total, level))
            if level < levels - 1:
                total = call(
                    functools.partial(join_kernel, functools.partial(bit, level), up),
                    f"join{'up' if up else 'down'}{level}", row, [VMEM] * 6, 8,
                    3 * count * flops, 2 << 20,
                )(total, heard[level], *own[level], *other[level])
        return heard

    partners = [part for pair in other for part in pair]
    heard = exchange(total, False)
    y, came, left, right = call(
        functools.partial(down_kernel, bits, levels), "down", (field, row, edge, edge),
        [VMEM] * (4 + levels + 2 * (levels - 1)), 16, 9 * layers * count * flops, 6 << 20,
    )(g, vert, inv_high, inv_low, *heard, *partners)
    low, high = from_sides(left, right)
    h, total = call(
        functools.partial(turn_kernel, place), "turn", (field, row), [VMEM] * 10, 8,
        3 * layers * count * flops, 4 << 20,
    )(y, came, rhs_field, low, high, neighbour_rows, weight, vert, inv_high, inv_low)
    heard = exchange(total, True)
    return call(
        functools.partial(up_kernel, bits, levels), "up", field,
        [VMEM] * (4 + levels + 2 * (levels - 1)), 16, 9 * layers * count * flops, 6 << 20,
    )(h, vert, inv_high, inv_low, *heard, *partners)


def solution(mesh):
    return jax.shard_map(
        shards,
        mesh=mesh,
        in_specs=(
            P("depth", None, "area"),
            P("depth", None, "area"),
            P("depth", "area", None),
            P("depth", "area"),
            P("area", None),
            P(),
            P(),
        ),
        out_specs=P("depth", None, "area"),
        check_vma=False,
    )
```
